512 devices in a mesh: dp: 4 (over x_hi, core), ctx: 64 (over y, z), head: 2 (over x_lo).
Axes of the slice: x: 4 (x_hi: 2, x_lo: 2; x = x_hi * 2 + x_lo), y: 4, z: 16, core: 2. Of those that a mesh axis runs over, the one named last changes fastest.
Arguments:
- tokens: bfloat16 [32768, 2688], P(('dp', 'ctx'), 'head'), parts along dimension 0, may hold values from -650 to 650
- input_gain: float32 [2688], replicated, may hold values from 0.1 to 1.9
- q_weight: bfloat16 [2688, 2048], P('ctx', 'head'), may hold values from -0.125 to 0.125
- key_matrix: bfloat16 [2688, 1024], P('ctx', 'head'), may hold values from -0.125 to 0.125
- value_matrix: bfloat16 [2688, 1024], P('ctx', 'head'), may hold values from -0.125 to 0.125
- q_gain: float32 [128], replicated, may hold values from 0.8 to 2.5
- k_gain: float32 [128], replicated, may hold values from 0.8 to 2.5
Outputs:
- attended: bfloat16 [32768, 2048], P(('dp', 'ctx'), 'head'), parts along dimension 0
The draws below stay inside these ranges and needn't reach their ends.
There are 4 independent parts, one for each index of `dp`. The reference program is written for one: setup_inputs(seed, part) draws one part's arguments, and reference() takes and returns one part's arrays. A program takes and returns all parts, laid end to end along the dimension named above; an argument that names none is the same for every part. Nothing has to cross between parts.
All inputs are finite; a program needn't handle non-finite values.
Results may differ from the reference program's by a relative error of at most 0.012.
Values may be sent and summed in bfloat16 or wider, within the bound.
A program may use at most 64 MiB of HBM per device.

```python
import math
import jax
import jax.numpy as jnp
from jax import lax

MODEL_WIDTH = 2688
QUERY_HEADS = 16
KEY_VALUE_HEADS = 8
HEAD_SIZE = 128
WINDOW = 1024
SLAB_POSITIONS = 128
SEQUENCE_LENGTH = 8192
N_CTX = 64


def draw_tokens(key, part):
    first_key, second_key, third_key = jax.random.split(key, 3)
    noise = jax.random.truncated_normal(first_key, -4.0, 4.0, (SEQUENCE_LENGTH, MODEL_WIDTH), jnp.float32)
    row_scale = jnp.exp(jax.random.uniform(second_key, (SEQUENCE_LENGTH, 1), jnp.float32, 0.0, math.log(10.0)))
    column_scale = jnp.exp(jax.random.uniform(third_key, (1, MODEL_WIDTH), jnp.float32, 0.0, math.log(10.0)))
    return (noise * row_scale * column_scale).astype(jnp.bfloat16)


def shard_levels(key, dims, pieces, least, top_value):
    def one(axis_at, shards_of):
        steps = jax.random.uniform(jax.random.fold_in(jax.random.fold_in(key, 6), axis_at), (shards_of,), jnp.float32, least / len(pieces), top_value / len(pieces))
        return jnp.repeat(jnp.exp(steps), dims[axis_at] // shards_of).reshape((-1,) + (1,) * (len(dims) - axis_at - 1))

    loudness = one(*pieces[0])
    for cut in pieces[1:]:
        loudness = loudness * one(*cut)
    return loudness


def scatter_about(own_key, dims, scale, most, shards=(), held_as=jnp.bfloat16):
    factor_of = shard_levels(own_key, dims, shards, -0.22, 0.18) if shards else 1.0
    array = jax.random.normal(own_key, dims, jnp.float32) * scale * factor_of
    return jnp.minimum(jnp.maximum(array, -most), most).astype(held_as)


def setup_inputs(seed: int = 0, part: int = 0) -> dict:
    key_list = jax.random.split(jax.random.key(seed), 8)
    part_splits = jax.random.split(jax.random.fold_in(key_list[7], part), 8)
    tokens = draw_tokens(jax.random.fold_in(jax.random.fold_in(key_list[7], part), 71), part)
    input_gain = jnp.clip(1.0 + 0.18 * jax.random.normal(key_list[1], (MODEL_WIDTH,), jnp.float32), 0.1, 1.9)
    q_weight = scatter_about(key_list[2], (MODEL_WIDTH, QUERY_HEADS * HEAD_SIZE), MODEL_WIDTH ** -0.5, 0.125, ((0, 64), (1, 2)))
    key_matrix = scatter_about(key_list[3], (MODEL_WIDTH, KEY_VALUE_HEADS * HEAD_SIZE), MODEL_WIDTH ** -0.5, 0.125, ((0, 64), (1, 2)))
    value_matrix = scatter_about(key_list[4], (MODEL_WIDTH, KEY_VALUE_HEADS * HEAD_SIZE), MODEL_WIDTH ** -0.5, 0.125, ((0, 64), (1, 2)))
    q_gain = jnp.clip(jnp.exp(jax.random.uniform(key_list[5], (HEAD_SIZE,), jnp.float32, math.log(0.8), math.log(2.5))), 0.8, 2.5)
    k_gain = jnp.clip(jnp.exp(jax.random.uniform(key_list[6], (HEAD_SIZE,), jnp.float32, math.log(0.8), math.log(2.5))), 0.8, 2.5)
    return {"tokens": tokens, "input_gain": input_gain, "q_weight": q_weight, "key_matrix": key_matrix, "value_matrix": value_matrix, "q_gain": q_gain, "k_gain": k_gain}


def head_norm(tensor, scales):
    mean_square = lax.optimization_barrier(jnp.mean(tensor * tensor, axis=-1, keepdims=True))
    return tensor * lax.rsqrt(mean_square + 1e-06) * scales

def rotate(tensor, positions):
    half_width = tensor.shape[-1] // 2
    frequency = jnp.exp(jnp.arange(half_width).astype(jnp.float32) * (-2.0 * math.log(10000.0) / tensor.shape[-1]))
    angles = positions.astype(jnp.float32)[:, None] * frequency[None, :]
    cosine = jnp.cos(angles)[:, None, :]
    sine_part = jnp.sin(angles)[:, None, :]
    first_half = tensor[..., :half_width]
    second_half = tensor[..., half_width:]
    return jnp.concatenate([first_half * cosine - second_half * sine_part, second_half * cosine + first_half * sine_part], axis=-1)

def reference(tokens, input_gain, q_weight, key_matrix, value_matrix, q_gain, k_gain):
    features = tokens.astype(jnp.float32)
    mean_square = lax.optimization_barrier(jnp.mean(features * features, axis=-1, keepdims=True))
    normalized_input = (features * lax.rsqrt(mean_square + 1e-06) * input_gain).astype(jnp.bfloat16)
    queries = jnp.dot(normalized_input, q_weight, preferred_element_type=jnp.float32).reshape(SEQUENCE_LENGTH, QUERY_HEADS, HEAD_SIZE)
    projected_key_rows = jnp.dot(normalized_input, key_matrix, preferred_element_type=jnp.float32).reshape(SEQUENCE_LENGTH, KEY_VALUE_HEADS, HEAD_SIZE)
    value_tensor = jnp.dot(normalized_input, value_matrix, preferred_element_type=jnp.float32).reshape(SEQUENCE_LENGTH, KEY_VALUE_HEADS, HEAD_SIZE)
    positions = jnp.arange(SEQUENCE_LENGTH, dtype=jnp.int32)
    scale = 1.0 / math.sqrt(168.0)
    rotary_queries = (rotate(head_norm(queries, q_gain), positions) * scale).astype(jnp.bfloat16)
    rotary_keys = rotate(head_norm(projected_key_rows, k_gain), positions).astype(jnp.bfloat16)
    projected_value_rows = value_tensor.astype(jnp.bfloat16)
    window_extent = WINDOW // SLAB_POSITIONS
    padded_keys = jnp.concatenate([jnp.zeros((window_extent * SLAB_POSITIONS, KEY_VALUE_HEADS, HEAD_SIZE), jnp.bfloat16), rotary_keys], axis=0)
    padded_values = jnp.concatenate([jnp.zeros((window_extent * SLAB_POSITIONS, KEY_VALUE_HEADS, HEAD_SIZE), jnp.bfloat16), projected_value_rows], axis=0)
    key_count = (window_extent + 1) * SLAB_POSITIONS
    head_groups = QUERY_HEADS // KEY_VALUE_HEADS

    def attend(block_index):
        leading_row = (block_index * SLAB_POSITIONS).astype(jnp.int32)
        query_tile_rows = lax.dynamic_slice_in_dim(rotary_queries, leading_row, SLAB_POSITIONS, 0).reshape(SLAB_POSITIONS, KEY_VALUE_HEADS, head_groups, HEAD_SIZE)
        key_block = lax.dynamic_slice_in_dim(padded_keys, leading_row, key_count, 0)
        value_block = lax.dynamic_slice_in_dim(padded_values, leading_row, key_count, 0)
        query_pos = leading_row + jnp.arange(SLAB_POSITIONS, dtype=jnp.int32)
        key_pos = leading_row - window_extent * SLAB_POSITIONS + jnp.arange(key_count, dtype=jnp.int32)
        allowed = (key_pos[None, :] <= query_pos[:, None]) & (key_pos[None, :] > query_pos[:, None] - WINDOW) & (key_pos[None, :] >= 0)
        scores = jnp.einsum('sgrd,lgd->grsl', query_tile_rows.astype(jnp.float32), key_block.astype(jnp.float32))
        unscaled = jnp.where(allowed[None, None], jnp.exp(scores), 0.0)
        totals = lax.optimization_barrier(jnp.sum(unscaled, axis=-1))
        weight_b = unscaled.astype(jnp.bfloat16)
        mixed = jnp.einsum('grsl,lgd->sgrd', weight_b.astype(jnp.float32), value_block.astype(jnp.float32))
        mixed = mixed / jnp.transpose(totals, (2, 0, 1))[..., None]
        return mixed.reshape(SLAB_POSITIONS, QUERY_HEADS * HEAD_SIZE).astype(jnp.bfloat16)
    blocks = lax.map(attend, jnp.arange(N_CTX, dtype=jnp.int32))
    return blocks.reshape(SEQUENCE_LENGTH, QUERY_HEADS * HEAD_SIZE)
```

```python
import math

import jax
import jax.numpy as jnp
from jax import lax
from jax.sharding import PartitionSpec as P

HEAD_SIZE = 128
WINDOW = 1024


def passed_along(x, axis):
    size = lax.axis_size(axis)
    pairs = [(i, i + 1) for i in range(size - 1)]
    return lax.ppermute(x, axis, pairs)


def head_norm(tensor, scales):
    mean_square = jnp.mean(tensor * tensor, axis=-1, keepdims=True)
    return tensor * lax.rsqrt(mean_square + 1e-06) * scales


def rotate(tensor, cosine, sine):
    half_width = tensor.shape[-1] // 2
    first_half = tensor[..., :half_width]
    second_half = tensor[..., half_width:]
    return jnp.concatenate(
        [
            first_half * cosine - second_half * sine,
            second_half * cosine + first_half * sine,
        ],
        axis=-1,
    )


def shards(tokens, input_gain, q_weight, key_matrix, value_matrix, q_gain, k_gain):
    sequences = lax.axis_size("dp")
    mine = lax.axis_index("dp")
    q_cols = q_weight.shape[1] // sequences
    k_cols = key_matrix.shape[1] // sequences
    weight_rows = jnp.concatenate(
        [
            lax.dynamic_slice_in_dim(q_weight, mine * q_cols, q_cols, 1),
            lax.dynamic_slice_in_dim(key_matrix, mine * k_cols, k_cols, 1),
            lax.dynamic_slice_in_dim(value_matrix, mine * k_cols, k_cols, 1),
        ],
        axis=1,
    )
    weights = lax.all_gather(weight_rows, "ctx", axis=0, tiled=True)

    row_count = tokens.shape[0]
    gathered = lax.all_gather(tokens, ("dp", "head"), axis=0, tiled=False)
    gathered = gathered.reshape(sequences, 2, row_count, tokens.shape[1])
    features = jnp.concatenate([gathered[:, 0], gathered[:, 1]], axis=-1).astype(jnp.float32)
    features = features.reshape(sequences * row_count, -1)
    mean_square = jnp.mean(features * features, axis=-1, keepdims=True)
    normalized = (features * lax.rsqrt(mean_square + 1e-06) * input_gain).astype(jnp.bfloat16)

    projected = jnp.dot(normalized, weights, preferred_element_type=jnp.float32)
    projected = projected.reshape(sequences, row_count, -1, HEAD_SIZE)
    groups = q_cols // HEAD_SIZE

    position = lax.axis_index("ctx")
    own_pos = position * row_count + jnp.arange(row_count, dtype=jnp.int32)
    frequency = jnp.exp(
        jnp.arange(HEAD_SIZE // 2).astype(jnp.float32) * (-2.0 * math.log(10000.0) / HEAD_SIZE)
    )
    angles = own_pos.astype(jnp.float32)[:, None] * frequency[None, :]
    cosine = jnp.cos(angles)
    sine = jnp.sin(angles)

    keys = rotate(head_norm(projected[:, :, groups], k_gain), cosine, sine).astype(jnp.bfloat16)
    values = projected[:, :, groups + 1].astype(jnp.bfloat16)
    scale = 1.0 / math.sqrt(168.0)
    queries = jnp.transpose(projected[:, :, :groups], (0, 2, 1, 3))
    queries = (rotate(head_norm(queries, q_gain), cosine, sine) * scale).astype(jnp.bfloat16)
    queries = queries.reshape(sequences, groups * row_count, HEAD_SIZE)

    local_q = (jnp.arange(groups * row_count, dtype=jnp.int32) % row_count)[:, None]
    local_k = jnp.arange(row_count, dtype=jnp.int32)[None, :]
    spans = WINDOW // row_count

    def partial(block, offset):
        key_part, value_part = block
        scores = jnp.einsum("brd,bkd->brk", queries, key_part, preferred_element_type=jnp.float32)
        if offset == 0:
            allowed = local_k <= local_q
        elif offset == spans:
            allowed = (local_k > local_q) & (position >= offset)
        else:
            allowed = jnp.broadcast_to(position >= offset, (groups * row_count, row_count))
        weight = jnp.where(allowed[None], jnp.exp(scores), 0.0)
        total = jnp.sum(weight, axis=-1, keepdims=True)
        mixed = jnp.einsum(
            "brk,bkd->brd",
            weight.astype(jnp.bfloat16),
            value_part,
            preferred_element_type=jnp.float32,
        )
        return mixed, total

    block = (keys, values)
    mixed = 0.0
    total = 0.0
    for offset in range(spans + 1):
        following = passed_along(block, "ctx") if offset < spans else None
        more, sums = partial(block, offset)
        mixed = mixed + more
        total = total + sums
        block = following

    attended = (mixed / total).astype(jnp.bfloat16)
    attended = attended.reshape(sequences, groups, row_count, HEAD_SIZE)
    returned = lax.all_to_all(attended, "dp", split_axis=0, concat_axis=0, tiled=True)
    return jnp.transpose(returned, (2, 0, 1, 3)).reshape(row_count, -1)


def solution(mesh):
    placed = (
        P(("dp", "ctx"), "head"),
        P(),
        P("ctx", "head"),
        P("ctx", "head"),
        P("ctx", "head"),
        P(),
        P(),
    )
    return jax.shard_map(
        shards, mesh=mesh, in_specs=placed, out_specs=P(("dp", "ctx"), "head"), check_vma=False
    )
```

```python
import math

import jax
import jax.numpy as jnp
from jax import lax
from jax.experimental import pallas as pl
from jax.experimental.pallas import tpu as pltpu
from jax.sharding import PartitionSpec as P

HEAD_SIZE = 128
WINDOW = 1024
RING = 16
LAG = 6


def passed_along(x, axis):
    size = lax.axis_size(axis)
    pairs = [(i, i + 1) for i in range(size - 1)]
    return lax.ppermute(x, axis, pairs)


def gather_kernel(rows_ref, tokens_ref, w_ref, t_ref, z_sems, y_sems, relay_sems, x_sems, pair_sems, own_sems):
    position = lax.axis_index("ctx")
    dp = lax.axis_index("dp")
    head = lax.axis_index("head")
    y = position // RING
    z = lax.rem(position, RING)
    column = w_ref.shape[0] // RING

    def at(row, along):
        return lax.rem(row + column, column) * RING + lax.rem(along + RING, RING)

    z_next = {"ctx": at(y, z + 1)}
    z_back = {"ctx": at(y, z - 1)}
    y_next = {"ctx": at(y + 1, z)}
    y_back = {"ctx": at(y - 1, z)}
    far = lax.rem(dp + 2, 4)
    other_dp = dp + 1 - 2 * lax.rem(dp, 2)
    other_far = far + 1 - 2 * lax.rem(far, 2)
    partner = {"dp": other_dp}
    peers = (
        {"head": 1 - head},
        {"dp": far, "head": 1 - head},
        {"dp": far},
    )
    slot = head * 4 + dp
    peer_slots = ((1 - head) * 4 + dp, (1 - head) * 4 + far, head * 4 + far)
    partner_slots = (
        head * 4 + other_dp,
        (1 - head) * 4 + other_dp,
        (1 - head) * 4 + other_far,
        head * 4 + other_far,
    )

    barrier = pltpu.get_barrier_semaphore()
    greeted = (z_next, z_back, y_next, y_back, partner) + peers
    for other in greeted:
        pl.semaphore_signal(barrier, inc=1, device_id=other, device_id_type=pl.DeviceIdType.MESH)
    pl.semaphore_wait(barrier, len(greeted))

    def remote(source, target, sems, index, device):
        return pltpu.make_async_remote_copy(
            src_ref=source,
            dst_ref=target,
            send_sem=sems.at[(0, *index)],
            recv_sem=sems.at[(1, *index)],
            device_id=device,
            device_id_type=pl.DeviceIdType.MESH,
        )

    along = [0]
    for step in range(1, RING // 2 + 1):
        along.append(-step)
        if step < RING // 2:
            along.append(step)

    own_w = pltpu.make_async_copy(rows_ref, w_ref.at[position], own_sems.at[0])
    own_t = pltpu.make_async_copy(tokens_ref, t_ref.at[slot], own_sems.at[1])
    own_w.start()
    own_t.start()
    sent = []

    def send(copy):
        copy.start()
        sent.append(copy)

    for n, other in enumerate(peers):
        send(remote(tokens_ref, t_ref.at[slot], x_sems, (n,), other))

    def relay(k):
        for way, device, row in ((0, y_next, y - 1), (1, y_back, y + 1)):
            arrived = w_ref.at[at(row, z + along[k])]
            remote(arrived, arrived, y_sems, (way, k), device).wait_recv()
            if way == k % 2:
                send(remote(arrived, arrived, relay_sems, (k,), device))

    for k in range(RING):
        block = w_ref.at[at(y, z + along[k])]
        if k == 0:
            source = rows_ref
            send(remote(source, block, z_sems, (1,), z_next))
            send(remote(source, block, z_sems, (2,), z_back))
        else:
            source = block
            remote(block, block, z_sems, (k,), z_next).wait_recv()
            if k + 2 < RING:
                send(remote(block, block, z_sems, (k + 2,), z_next if k % 2 else z_back))
        send(remote(source, block, y_sems, (0, k), y_next))
        send(remote(source, block, y_sems, (1, k), y_back))
        if k == 0:
            send(remote(tokens_ref, t_ref.at[slot], pair_sems, (0,), partner))
        if k == 9:
            for n, from_slot in enumerate(peer_slots):
                arrived = t_ref.at[from_slot]
                remote(arrived, arrived, x_sems, (n,), peers[n]).wait_recv()
                send(remote(arrived, arrived, pair_sems, (n + 1,), partner))
        if k >= LAG:
            relay(k - LAG)
    for k in range(RING - LAG, RING):
        relay(k)
    for k in range(RING):
        arrived = w_ref.at[at(y + 2, z + along[k])]
        remote(arrived, arrived, relay_sems, (k,), y_next).wait_recv()
    for n, from_slot in enumerate(partner_slots):
        arrived = t_ref.at[from_slot]
        remote(arrived, arrived, pair_sems, (n,), partner).wait_recv()
    own_w.wait()
    own_t.wait()
    for copy in sent:
        copy.wait_send()


def gather_all(weight_rows, tokens):
    count = lax.axis_size("ctx")
    vmem = pl.BlockSpec(memory_space=pltpu.VMEM)
    return pl.pallas_call(
        gather_kernel,
        out_shape=(
            jax.ShapeDtypeStruct((count, *weight_rows.shape), weight_rows.dtype),
            jax.ShapeDtypeStruct((8, *tokens.shape), tokens.dtype),
        ),
        in_specs=[vmem, vmem],
        out_specs=(vmem, vmem),
        scratch_shapes=[
            pltpu.SemaphoreType.DMA((2, RING)),
            pltpu.SemaphoreType.DMA((2, 2, RING)),
            pltpu.SemaphoreType.DMA((2, RING)),
            pltpu.SemaphoreType.DMA((2, 3)),
            pltpu.SemaphoreType.DMA((2, 4)),
            pltpu.SemaphoreType.DMA((2,)),
        ],
        compiler_params=pltpu.CompilerParams(collective_id=0, has_side_effects=True),
    )(weight_rows, tokens)


def head_norm(tensor, scales):
    mean_square = jnp.mean(tensor * tensor, axis=-1, keepdims=True)
    return tensor * lax.rsqrt(mean_square + 1e-06) * scales


def rotate(tensor, cosine, sine):
    half_width = tensor.shape[-1] // 2
    first_half = tensor[..., :half_width]
    second_half = tensor[..., half_width:]
    return jnp.concatenate(
        [
            first_half * cosine - second_half * sine,
            second_half * cosine + first_half * sine,
        ],
        axis=-1,
    )


def shards(tokens, input_gain, q_weight, key_matrix, value_matrix, q_gain, k_gain):
    sequences = lax.axis_size("dp")
    mine = lax.axis_index("dp")
    q_cols = q_weight.shape[1] // sequences
    k_cols = key_matrix.shape[1] // sequences
    weight_rows = jnp.concatenate(
        [
            lax.dynamic_slice_in_dim(q_weight, mine * q_cols, q_cols, 1),
            lax.dynamic_slice_in_dim(key_matrix, mine * k_cols, k_cols, 1),
            lax.dynamic_slice_in_dim(value_matrix, mine * k_cols, k_cols, 1),
        ],
        axis=1,
    )
    weights, gathered = gather_all(weight_rows, tokens)
    weights = weights.reshape(2, tokens.shape[1], -1)

    row_count = tokens.shape[0]
    features = gathered.reshape(2, sequences * row_count, -1).astype(jnp.float32)
    width = 2 * tokens.shape[1]
    mean_square = jnp.sum(features * features, axis=(0, 2)) / width
    factor = lax.rsqrt(mean_square + 1e-06)[None, :, None]
    gains = input_gain.reshape(2, 1, -1)
    normalized = (features * factor * gains).astype(jnp.bfloat16)

    projected = jnp.dot(normalized[0], weights[0], preferred_element_type=jnp.float32)
    projected += jnp.dot(normalized[1], weights[1], preferred_element_type=jnp.float32)
    projected = projected.reshape(sequences, row_count, -1, HEAD_SIZE)
    groups = q_cols // HEAD_SIZE

    position = lax.axis_index("ctx")
    own_pos = position * row_count + jnp.arange(row_count, dtype=jnp.int32)
    frequency = jnp.exp(
        jnp.arange(HEAD_SIZE // 2).astype(jnp.float32) * (-2.0 * math.log(10000.0) / HEAD_SIZE)
    )
    angles = own_pos.astype(jnp.float32)[:, None] * frequency[None, :]
    cosine = jnp.cos(angles)
    sine = jnp.sin(angles)

    keys = rotate(head_norm(projected[:, :, groups], k_gain), cosine, sine).astype(jnp.bfloat16)
    values = projected[:, :, groups + 1].astype(jnp.bfloat16)
    scale = 1.0 / math.sqrt(168.0)
    queries = jnp.transpose(projected[:, :, :groups], (0, 2, 1, 3))
    queries = (rotate(head_norm(queries, q_gain), cosine, sine) * scale).astype(jnp.bfloat16)
    queries = queries.reshape(sequences, groups * row_count, HEAD_SIZE)

    local_q = (jnp.arange(groups * row_count, dtype=jnp.int32) % row_count)[:, None]
    local_k = jnp.arange(row_count, dtype=jnp.int32)[None, :]
    spans = WINDOW // row_count

    def partial(block, offset):
        key_part, value_part = block
        scores = jnp.einsum("brd,bkd->brk", queries, key_part, preferred_element_type=jnp.float32)
        if offset == 0:
            allowed = local_k <= local_q
        elif offset == spans:
            allowed = (local_k > local_q) & (position >= offset)
        else:
            allowed = jnp.broadcast_to(position >= offset, (groups * row_count, row_count))
        weight = jnp.where(allowed[None], jnp.exp(scores), 0.0)
        total = jnp.sum(weight, axis=-1, keepdims=True)
        mixed = jnp.einsum(
            "brk,bkd->brd",
            weight.astype(jnp.bfloat16),
            value_part,
            preferred_element_type=jnp.float32,
        )
        return mixed, total

    block = (keys, values)
    mixed = 0.0
    total = 0.0
    for offset in range(spans + 1):
        following = passed_along(block, "ctx") if offset < spans else None
        more, sums = partial(block, offset)
        mixed = mixed + more
        total = total + sums
        block = following

    attended = (mixed / total).astype(jnp.bfloat16)
    attended = attended.reshape(sequences, groups, row_count, HEAD_SIZE)
    returned = lax.all_to_all(attended, "dp", split_axis=0, concat_axis=0, tiled=True)
    return jnp.transpose(returned, (2, 0, 1, 3)).reshape(row_count, -1)


def solution(mesh):
    placed = (
        P(("dp", "ctx"), "head"),
        P(),
        P("ctx", "head"),
        P("ctx", "head"),
        P("ctx", "head"),
        P(),
        P(),
    )
    return jax.shard_map(
        shards, mesh=mesh, in_specs=placed, out_specs=P(("dp", "ctx"), "head"), check_vma=False
    )
```

```python
import math

import jax
import jax.numpy as jnp
from jax import lax
from jax.experimental import pallas as pl
from jax.experimental.pallas import tpu as pltpu
from jax.sharding import PartitionSpec as P

HEAD_SIZE = 128
WINDOW = 1024
RING = 16
LAG = 6


def window_kernel(q_ref, kv_ref, o_ref, held, mixed, total, sems):
    position = lax.axis_index("ctx")
    size = lax.axis_size("ctx")
    behind = {"ctx": lax.rem(position + size - 1, size)}
    ahead = {"ctx": lax.rem(position + 1, size)}
    barrier = pltpu.get_barrier_semaphore()
    for other in (behind, ahead):
        pl.semaphore_signal(barrier, inc=1, device_id=other, device_id_type=pl.DeviceIdType.MESH)
    pl.semaphore_wait(barrier, 2)
    spans = held.shape[0]
    sequences, rows, _ = q_ref.shape
    keys = kv_ref.shape[2]
    local_q = lax.rem(lax.broadcasted_iota(jnp.int32, (rows, keys), 0), keys)
    local_k = lax.broadcasted_iota(jnp.int32, (rows, keys), 1)
    sent = []

    def hop(offset, part, source):
        return pltpu.make_async_remote_copy(
            src_ref=source,
            dst_ref=held.at[offset, part],
            send_sem=sems.at[0, offset, part],
            recv_sem=sems.at[1, offset, part],
            device_id=ahead,
            device_id_type=pl.DeviceIdType.MESH,
        )

    for part in range(2):
        copy = hop(0, part, kv_ref.at[part])
        copy.start()
        sent.append(copy)
    for offset in range(spans + 1):
        block = kv_ref
        if offset:
            block = held.at[offset - 1]
            for part in range(2):
                hop(offset - 1, part, block.at[part]).wait_recv()
                if offset < spans:
                    copy = hop(offset, part, block.at[part])
                    copy.start()
                    sent.append(copy)
        if offset == 0:
            allowed = local_k <= local_q
        elif offset == spans:
            allowed = (local_k > local_q) & (position >= offset)
        else:
            allowed = (local_k >= 0) & (position >= offset)
        for b in range(sequences):
            scores = lax.dot_general(
                q_ref[b],
                block[0, b],
                (((1,), (1,)), ((), ())),
                preferred_element_type=jnp.float32,
            )
            weight = jnp.where(allowed, jnp.exp(scores), 0.0)
            sums = jnp.sum(weight, axis=-1, keepdims=True)
            more = jnp.dot(
                weight.astype(jnp.bfloat16), block[1, b], preferred_element_type=jnp.float32
            )
            if offset == 0:
                total[b] = sums
                mixed[b] = more
            else:
                total[b] += sums
                mixed[b] += more
    for b in range(sequences):
        o_ref[b] = (mixed[b] / total[b]).astype(o_ref.dtype)
    for copy in sent:
        copy.wait_send()


def attend(queries, block):
    vmem = pl.BlockSpec(memory_space=pltpu.VMEM)
    sequences, rows, _ = queries.shape
    spans = WINDOW // block.shape[2]
    return pl.pallas_call(
        window_kernel,
        out_shape=jax.ShapeDtypeStruct(queries.shape, queries.dtype),
        in_specs=[vmem, vmem],
        out_specs=vmem,
        scratch_shapes=[
            pltpu.VMEM((spans, *block.shape), block.dtype),
            pltpu.VMEM(queries.shape, jnp.float32),
            pltpu.VMEM((sequences, rows, 1), jnp.float32),
            pltpu.SemaphoreType.DMA((2, spans, 2)),
        ],
        compiler_params=pltpu.CompilerParams(collective_id=1, has_side_effects=True),
    )(queries, block)


def gather_kernel(rows_ref, tokens_ref, w_ref, t_ref, z_sems, y_sems, relay_sems, x_sems, pair_sems, own_sems):
    position = lax.axis_index("ctx")
    dp = lax.axis_index("dp")
    head = lax.axis_index("head")
    y = position // RING
    z = lax.rem(position, RING)
    column = w_ref.shape[0] // RING

    def at(row, along):
        return lax.rem(row + column, column) * RING + lax.rem(along + RING, RING)

    z_next = {"ctx": at(y, z + 1)}
    z_back = {"ctx": at(y, z - 1)}
    y_next = {"ctx": at(y + 1, z)}
    y_back = {"ctx": at(y - 1, z)}
    far = lax.rem(dp + 2, 4)
    other_dp = dp + 1 - 2 * lax.rem(dp, 2)
    other_far = far + 1 - 2 * lax.rem(far, 2)
    partner = {"dp": other_dp}
    peers = (
        {"head": 1 - head},
        {"dp": far, "head": 1 - head},
        {"dp": far},
    )
    slot = head * 4 + dp
    peer_slots = ((1 - head) * 4 + dp, (1 - head) * 4 + far, head * 4 + far)
    partner_slots = (
        head * 4 + other_dp,
        (1 - head) * 4 + other_dp,
        (1 - head) * 4 + other_far,
        head * 4 + other_far,
    )

    barrier = pltpu.get_barrier_semaphore()
    greeted = (z_next, z_back, y_next, y_back, partner) + peers
    for other in greeted:
        pl.semaphore_signal(barrier, inc=1, device_id=other, device_id_type=pl.DeviceIdType.MESH)
    pl.semaphore_wait(barrier, len(greeted))

    def remote(source, target, sems, index, device):
        return pltpu.make_async_remote_copy(
            src_ref=source,
            dst_ref=target,
            send_sem=sems.at[(0, *index)],
            recv_sem=sems.at[(1, *index)],
            device_id=device,
            device_id_type=pl.DeviceIdType.MESH,
        )

    along = [0]
    for step in range(1, RING // 2 + 1):
        along.append(-step)
        if step < RING // 2:
            along.append(step)

    own_w = pltpu.make_async_copy(rows_ref, w_ref.at[position], own_sems.at[0])
    own_t = pltpu.make_async_copy(tokens_ref, t_ref.at[slot], own_sems.at[1])
    own_w.start()
    own_t.start()
    sent = []

    def send(copy):
        copy.start()
        sent.append(copy)

    for n, other in enumerate(peers):
        send(remote(tokens_ref, t_ref.at[slot], x_sems, (n,), other))

    def relay(k):
        for way, device, row in ((0, y_next, y - 1), (1, y_back, y + 1)):
            arrived = w_ref.at[at(row, z + along[k])]
            remote(arrived, arrived, y_sems, (way, k), device).wait_recv()
            if way == k % 2:
                send(remote(arrived, arrived, relay_sems, (k,), device))

    for k in range(RING):
        block = w_ref.at[at(y, z + along[k])]
        if k == 0:
            source = rows_ref
            send(remote(source, block, z_sems, (1,), z_next))
            send(remote(source, block, z_sems, (2,), z_back))
        else:
            source = block
            remote(block, block, z_sems, (k,), z_next).wait_recv()
            if k + 2 < RING:
                send(remote(block, block, z_sems, (k + 2,), z_next if k % 2 else z_back))
        send(remote(source, block, y_sems, (0, k), y_next))
        send(remote(source, block, y_sems, (1, k), y_back))
        if k == 0:
            send(remote(tokens_ref, t_ref.at[slot], pair_sems, (0,), partner))
        if k == 9:
            for n, from_slot in enumerate(peer_slots):
                arrived = t_ref.at[from_slot]
                remote(arrived, arrived, x_sems, (n,), peers[n]).wait_recv()
                send(remote(arrived, arrived, pair_sems, (n + 1,), partner))
        if k >= LAG:
            relay(k - LAG)
    for k in range(RING - LAG, RING):
        relay(k)
    for k in range(RING):
        arrived = w_ref.at[at(y + 2, z + along[k])]
        remote(arrived, arrived, relay_sems, (k,), y_next).wait_recv()
    for n, from_slot in enumerate(partner_slots):
        arrived = t_ref.at[from_slot]
        remote(arrived, arrived, pair_sems, (n,), partner).wait_recv()
    own_w.wait()
    own_t.wait()
    for copy in sent:
        copy.wait_send()


def gather_all(weight_rows, tokens):
    count = lax.axis_size("ctx")
    vmem = pl.BlockSpec(memory_space=pltpu.VMEM)
    return pl.pallas_call(
        gather_kernel,
        out_shape=(
            jax.ShapeDtypeStruct((count, *weight_rows.shape), weight_rows.dtype),
            jax.ShapeDtypeStruct((8, *tokens.shape), tokens.dtype),
        ),
        in_specs=[vmem, vmem],
        out_specs=(vmem, vmem),
        scratch_shapes=[
            pltpu.SemaphoreType.DMA((2, RING)),
            pltpu.SemaphoreType.DMA((2, 2, RING)),
            pltpu.SemaphoreType.DMA((2, RING)),
            pltpu.SemaphoreType.DMA((2, 3)),
            pltpu.SemaphoreType.DMA((2, 4)),
            pltpu.SemaphoreType.DMA((2,)),
        ],
        compiler_params=pltpu.CompilerParams(collective_id=0, has_side_effects=True),
    )(weight_rows, tokens)


def head_norm(tensor, scales):
    mean_square = jnp.mean(tensor * tensor, axis=-1, keepdims=True)
    return tensor * lax.rsqrt(mean_square + 1e-06) * scales


def rotate(tensor, cosine, sine):
    half_width = tensor.shape[-1] // 2
    first_half = tensor[..., :half_width]
    second_half = tensor[..., half_width:]
    return jnp.concatenate(
        [
            first_half * cosine - second_half * sine,
            second_half * cosine + first_half * sine,
        ],
        axis=-1,
    )


def shards(tokens, input_gain, q_weight, key_matrix, value_matrix, q_gain, k_gain):
    sequences = lax.axis_size("dp")
    mine = lax.axis_index("dp")
    q_cols = q_weight.shape[1] // sequences
    k_cols = key_matrix.shape[1] // sequences
    weight_rows = jnp.concatenate(
        [
            lax.dynamic_slice_in_dim(q_weight, mine * q_cols, q_cols, 1),
            lax.dynamic_slice_in_dim(key_matrix, mine * k_cols, k_cols, 1),
            lax.dynamic_slice_in_dim(value_matrix, mine * k_cols, k_cols, 1),
        ],
        axis=1,
    )
    weights, gathered = gather_all(weight_rows, tokens)
    weights = weights.reshape(2, tokens.shape[1], -1)

    row_count = tokens.shape[0]
    features = gathered.reshape(2, sequences * row_count, -1).astype(jnp.float32)
    width = 2 * tokens.shape[1]
    mean_square = jnp.sum(features * features, axis=(0, 2)) / width
    factor = lax.rsqrt(mean_square + 1e-06)[None, :, None]
    gains = input_gain.reshape(2, 1, -1)
    normalized = (features * factor * gains).astype(jnp.bfloat16)

    projected = jnp.dot(normalized[0], weights[0], preferred_element_type=jnp.float32)
    projected += jnp.dot(normalized[1], weights[1], preferred_element_type=jnp.float32)
    projected = projected.reshape(sequences, row_count, -1, HEAD_SIZE)
    groups = q_cols // HEAD_SIZE

    position = lax.axis_index("ctx")
    own_pos = position * row_count + jnp.arange(row_count, dtype=jnp.int32)
    frequency = jnp.exp(
        jnp.arange(HEAD_SIZE // 2).astype(jnp.float32) * (-2.0 * math.log(10000.0) / HEAD_SIZE)
    )
    angles = own_pos.astype(jnp.float32)[:, None] * frequency[None, :]
    cosine = jnp.cos(angles)
    sine = jnp.sin(angles)

    keys = rotate(head_norm(projected[:, :, groups], k_gain), cosine, sine).astype(jnp.bfloat16)
    values = projected[:, :, groups + 1].astype(jnp.bfloat16)
    scale = 1.0 / math.sqrt(168.0)
    queries = jnp.transpose(projected[:, :, :groups], (0, 2, 1, 3))
    queries = (rotate(head_norm(queries, q_gain), cosine, sine) * scale).astype(jnp.bfloat16)
    queries = queries.reshape(sequences, groups * row_count, HEAD_SIZE)

    attended = attend(queries, jnp.stack([keys, values]))
    attended = attended.reshape(sequences, groups, row_count, HEAD_SIZE)
    returned = lax.all_to_all(attended, "dp", split_axis=0, concat_axis=0, tiled=True)
    return jnp.transpose(returned, (2, 0, 1, 3)).reshape(row_count, -1)


def solution(mesh):
    placed = (
        P(("dp", "ctx"), "head"),
        P(),
        P("ctx", "head"),
        P("ctx", "head"),
        P("ctx", "head"),
        P(),
        P(),
    )
    return jax.shard_map(
        shards, mesh=mesh, in_specs=placed, out_specs=P(("dp", "ctx"), "head"), check_vma=False
    )
```

```python
import math

import jax
import jax.numpy as jnp
from jax import lax
from jax.experimental import pallas as pl
from jax.experimental.pallas import tpu as pltpu
from jax.sharding import PartitionSpec as P

HEAD_SIZE = 128
WINDOW = 1024
RING = 16
LAG = 6


def window_kernel(q_ref, kv_ref, o_ref, held, mixed, total, sems):
    position = lax.axis_index("ctx")
    size = lax.axis_size("ctx")
    behind = {"ctx": lax.rem(position + size - 1, size)}
    ahead = {"ctx": lax.rem(position + 1, size)}
    barrier = pltpu.get_barrier_semaphore()
    for other in (behind, ahead):
        pl.semaphore_signal(barrier, inc=1, device_id=other, device_id_type=pl.DeviceIdType.MESH)
    pl.semaphore_wait(barrier, 2)
    spans = held.shape[0]
    sequences, rows, _ = q_ref.shape
    keys = kv_ref.shape[2]
    local_q = lax.rem(lax.broadcasted_iota(jnp.int32, (rows, keys), 0), keys)
    local_k = lax.broadcasted_iota(jnp.int32, (rows, keys), 1)
    sent = []

    def hop(offset, part, source):
        return pltpu.make_async_remote_copy(
            src_ref=source,
            dst_ref=held.at[offset, part],
            send_sem=sems.at[0, offset, part],
            recv_sem=sems.at[1, offset, part],
            device_id=ahead,
            device_id_type=pl.DeviceIdType.MESH,
        )

    for part in range(2):
        copy = hop(0, part, kv_ref.at[part])
        copy.start()
        sent.append(copy)
    for offset in range(spans + 1):
        block = kv_ref
        if offset:
            block = held.at[offset - 1]
            for part in range(2):
                hop(offset - 1, part, block.at[part]).wait_recv()
                if offset < spans:
                    copy = hop(offset, part, block.at[part])
                    copy.start()
                    sent.append(copy)
        if offset == 0:
            allowed = local_k <= local_q
        elif offset == spans:
            allowed = (local_k > local_q) & (position >= offset)
        else:
            allowed = (local_k >= 0) & (position >= offset)
        for b in range(sequences):
            scores = lax.dot_general(
                q_ref[b],
                block[0, b],
                (((1,), (1,)), ((), ())),
                preferred_element_type=jnp.float32,
            )
            weight = jnp.where(allowed, jnp.exp(scores), 0.0)
            sums = jnp.sum(weight, axis=-1, keepdims=True)
            more = jnp.dot(
                weight.astype(jnp.bfloat16), block[1, b], preferred_element_type=jnp.float32
            )
            if offset == 0:
                total[b] = sums
                mixed[b] = more
            else:
                total[b] += sums
                mixed[b] += more
    for b in range(sequences):
        o_ref[b] = (mixed[b] / total[b]).astype(o_ref.dtype)
    for copy in sent:
        copy.wait_send()


def attend(queries, block):
    vmem = pl.BlockSpec(memory_space=pltpu.VMEM)
    sequences, rows, _ = queries.shape
    spans = WINDOW // block.shape[2]
    return pl.pallas_call(
        window_kernel,
        out_shape=jax.ShapeDtypeStruct(queries.shape, queries.dtype),
        in_specs=[vmem, vmem],
        out_specs=vmem,
        scratch_shapes=[
            pltpu.VMEM((spans, *block.shape), block.dtype),
            pltpu.VMEM(queries.shape, jnp.float32),
            pltpu.VMEM((sequences, rows, 1), jnp.float32),
            pltpu.SemaphoreType.DMA((2, spans, 2)),
        ],
        compiler_params=pltpu.CompilerParams(collective_id=1, has_side_effects=True),
    )(queries, block)


def gather_kernel(rows_ref, tokens_ref, w_ref, t_ref, z_sems, y_sems, relay_sems, x_sems, pair_sems, own_sems):
    position = lax.axis_index("ctx")
    dp = lax.axis_index("dp")
    head = lax.axis_index("head")
    y = position // RING
    z = lax.rem(position, RING)
    column = w_ref.shape[0] // RING

    def at(row, along):
        return lax.rem(row + column, column) * RING + lax.rem(along + RING, RING)

    z_next = {"ctx": at(y, z + 1)}
    z_back = {"ctx": at(y, z - 1)}
    y_next = {"ctx": at(y + 1, z)}
    y_back = {"ctx": at(y - 1, z)}
    far = lax.rem(dp + 2, 4)
    other_dp = dp + 1 - 2 * lax.rem(dp, 2)
    other_far = far + 1 - 2 * lax.rem(far, 2)
    partner = {"dp": other_dp}
    peers = (
        {"head": 1 - head},
        {"dp": far, "head": 1 - head},
        {"dp": far},
    )
    slot = head * 4 + dp
    peer_slots = ((1 - head) * 4 + dp, (1 - head) * 4 + far, head * 4 + far)
    partner_slots = (
        head * 4 + other_dp,
        (1 - head) * 4 + other_dp,
        (1 - head) * 4 + other_far,
        head * 4 + other_far,
    )

    barrier = pltpu.get_barrier_semaphore()
    greeted = (z_next, z_back, y_next, y_back, partner) + peers
    for other in greeted:
        pl.semaphore_signal(barrier, inc=1, device_id=other, device_id_type=pl.DeviceIdType.MESH)
    pl.semaphore_wait(barrier, len(greeted))

    def remote(source, target, sems, index, device):
        return pltpu.make_async_remote_copy(
            src_ref=source,
            dst_ref=target,
            send_sem=sems.at[(0, *index)],
            recv_sem=sems.at[(1, *index)],
            device_id=device,
            device_id_type=pl.DeviceIdType.MESH,
        )

    along = [0]
    for step in range(1, RING // 2 + 1):
        along.append(-step)
        if step < RING // 2:
            along.append(step)

    own_w = pltpu.make_async_copy(rows_ref, w_ref.at[position], own_sems.at[0])
    own_t = pltpu.make_async_copy(tokens_ref, t_ref.at[slot], own_sems.at[1])
    own_w.start()
    own_t.start()
    sent = []

    def send(copy):
        copy.start()
        sent.append(copy)

    for n, other in enumerate(peers):
        send(remote(tokens_ref, t_ref.at[slot], x_sems, (n,), other))

    def relay(k):
        for way, device, row in ((0, y_next, y - 1), (1, y_back, y + 1)):
            arrived = w_ref.at[at(row, z + along[k])]
            remote(arrived, arrived, y_sems, (way, k), device).wait_recv()
            if way == k % 2:
                send(remote(arrived, arrived, relay_sems, (k,), device))

    for k in range(RING):
        block = w_ref.at[at(y, z + along[k])]
        if k == 0:
            source = rows_ref
            send(remote(source, block, z_sems, (1,), z_next))
            send(remote(source, block, z_sems, (2,), z_back))
        else:
            source = block
            remote(block, block, z_sems, (k,), z_next).wait_recv()
            if k + 2 < RING:
                send(remote(block, block, z_sems, (k + 2,), z_next if k % 2 else z_back))
        send(remote(source, block, y_sems, (0, k), y_next))
        send(remote(source, block, y_sems, (1, k), y_back))
        if k == 0:
            send(remote(tokens_ref, t_ref.at[slot], pair_sems, (0,), partner))
        if k == 9:
            for n, from_slot in enumerate(peer_slots):
                arrived = t_ref.at[from_slot]
                remote(arrived, arrived, x_sems, (n,), peers[n]).wait_recv()
                send(remote(arrived, arrived, pair_sems, (n + 1,), partner))
        if k >= LAG:
            relay(k - LAG)
    for k in range(RING - LAG, RING):
        relay(k)
    for k in range(RING):
        arrived = w_ref.at[at(y + 2, z + along[k])]
        remote(arrived, arrived, relay_sems, (k,), y_next).wait_recv()
    for n, from_slot in enumerate(partner_slots):
        arrived = t_ref.at[from_slot]
        remote(arrived, arrived, pair_sems, (n,), partner).wait_recv()
    own_w.wait()
    own_t.wait()
    for copy in sent:
        copy.wait_send()


def gather_all(weight_rows, tokens):
    count = lax.axis_size("ctx")
    vmem = pl.BlockSpec(memory_space=pltpu.VMEM)
    return pl.pallas_call(
        gather_kernel,
        out_shape=(
            jax.ShapeDtypeStruct((count, *weight_rows.shape), weight_rows.dtype),
            jax.ShapeDtypeStruct((8, *tokens.shape), tokens.dtype),
        ),
        in_specs=[vmem, vmem],
        out_specs=(vmem, vmem),
        scratch_shapes=[
            pltpu.SemaphoreType.DMA((2, RING)),
            pltpu.SemaphoreType.DMA((2, 2, RING)),
            pltpu.SemaphoreType.DMA((2, RING)),
            pltpu.SemaphoreType.DMA((2, 3)),
            pltpu.SemaphoreType.DMA((2, 4)),
            pltpu.SemaphoreType.DMA((2,)),
        ],
        compiler_params=pltpu.CompilerParams(collective_id=0, has_side_effects=True),
    )(weight_rows, tokens)


def return_kernel(in_ref, out_ref, sems, own_sem):
    dp = lax.axis_index("dp")
    count = in_ref.shape[0]
    barrier = pltpu.get_barrier_semaphore()
    others = [lax.rem(dp + d, count) for d in range(1, count)]
    for other in others:
        pl.semaphore_signal(
            barrier, inc=1, device_id={"dp": other}, device_id_type=pl.DeviceIdType.MESH
        )
    pl.semaphore_wait(barrier, count - 1)

    def remote(n, source, target):
        return pltpu.make_async_remote_copy(
            src_ref=in_ref.at[source],
            dst_ref=out_ref.at[target],
            send_sem=sems.at[0, n],
            recv_sem=sems.at[1, n],
            device_id={"dp": others[n]},
            device_id_type=pl.DeviceIdType.MESH,
        )

    sent = [remote(n, others[n], dp) for n in range(count - 1)]
    for copy in sent:
        copy.start()
    own = pltpu.make_async_copy(in_ref.at[dp], out_ref.at[dp], own_sem)
    own.start()
    for n in range(count - 1):
        source = lax.rem(dp + count - 1 - n, count)
        remote(n, source, source).wait_recv()
    own.wait()
    for copy in sent:
        copy.wait_send()


def give_back(attended):
    vmem = pl.BlockSpec(memory_space=pltpu.VMEM)
    count = attended.shape[0]
    return pl.pallas_call(
        return_kernel,
        out_shape=jax.ShapeDtypeStruct(attended.shape, attended.dtype),
        in_specs=[vmem],
        out_specs=vmem,
        scratch_shapes=[
            pltpu.SemaphoreType.DMA((2, count - 1)),
            pltpu.SemaphoreType.DMA,
        ],
        compiler_params=pltpu.CompilerParams(collective_id=2, has_side_effects=True),
    )(attended)


def head_norm(tensor, scales):
    mean_square = jnp.mean(tensor * tensor, axis=-1, keepdims=True)
    return tensor * lax.rsqrt(mean_square + 1e-06) * scales


def rotate(tensor, cosine, sine):
    half_width = tensor.shape[-1] // 2
    first_half = tensor[..., :half_width]
    second_half = tensor[..., half_width:]
    return jnp.concatenate(
        [
            first_half * cosine - second_half * sine,
            second_half * cosine + first_half * sine,
        ],
        axis=-1,
    )


def shards(tokens, input_gain, q_weight, key_matrix, value_matrix, q_gain, k_gain):
    sequences = lax.axis_size("dp")
    mine = lax.axis_index("dp")
    q_cols = q_weight.shape[1] // sequences
    k_cols = key_matrix.shape[1] // sequences
    weight_rows = jnp.concatenate(
        [
            lax.dynamic_slice_in_dim(q_weight, mine * q_cols, q_cols, 1),
            lax.dynamic_slice_in_dim(key_matrix, mine * k_cols, k_cols, 1),
            lax.dynamic_slice_in_dim(value_matrix, mine * k_cols, k_cols, 1),
        ],
        axis=1,
    )
    weights, gathered = gather_all(weight_rows, tokens)
    weights = weights.reshape(2, tokens.shape[1], -1)

    row_count = tokens.shape[0]
    features = gathered.reshape(2, sequences * row_count, -1).astype(jnp.float32)
    width = 2 * tokens.shape[1]
    mean_square = jnp.sum(features * features, axis=(0, 2)) / width
    factor = lax.rsqrt(mean_square + 1e-06)[None, :, None]
    gains = input_gain.reshape(2, 1, -1)
    normalized = (features * factor * gains).astype(jnp.bfloat16)

    projected = jnp.dot(normalized[0], weights[0], preferred_element_type=jnp.float32)
    projected += jnp.dot(normalized[1], weights[1], preferred_element_type=jnp.float32)
    projected = projected.reshape(sequences, row_count, -1, HEAD_SIZE)
    groups = q_cols // HEAD_SIZE

    position = lax.axis_index("ctx")
    own_pos = position * row_count + jnp.arange(row_count, dtype=jnp.int32)
    frequency = jnp.exp(
        jnp.arange(HEAD_SIZE // 2).astype(jnp.float32) * (-2.0 * math.log(10000.0) / HEAD_SIZE)
    )
    angles = own_pos.astype(jnp.float32)[:, None] * frequency[None, :]
    cosine = jnp.cos(angles)
    sine = jnp.sin(angles)

    keys = rotate(head_norm(projected[:, :, groups], k_gain), cosine, sine).astype(jnp.bfloat16)
    values = projected[:, :, groups + 1].astype(jnp.bfloat16)
    scale = 1.0 / math.sqrt(168.0)
    queries = jnp.transpose(projected[:, :, :groups], (0, 2, 1, 3))
    queries = (rotate(head_norm(queries, q_gain), cosine, sine) * scale).astype(jnp.bfloat16)
    queries = queries.reshape(sequences, groups * row_count, HEAD_SIZE)

    attended = attend(queries, jnp.stack([keys, values]))
    attended = attended.reshape(sequences, groups, row_count, HEAD_SIZE)
    returned = give_back(attended)
    return jnp.transpose(returned, (2, 0, 1, 3)).reshape(row_count, -1)


def solution(mesh):
    placed = (
        P(("dp", "ctx"), "head"),
        P(),
        P("ctx", "head"),
        P("ctx", "head"),
        P("ctx", "head"),
        P(),
        P(),
    )
    return jax.shard_map(
        shards, mesh=mesh, in_specs=placed, out_specs=P(("dp", "ctx"), "head"), check_vma=False
    )
```
